512 devices in a mesh: blk: 64 (over y, x, z_lo), rep: 8 (over z_hi, core).
Axes of the slice: x: 4, y: 8, z: 8 (z_hi: 4, z_lo: 2; z = z_hi * 2 + z_lo), core: 2. Of those that a mesh axis runs over, the one named last changes fastest.
Arguments:
- features: bfloat16 [65536, 256], P(('blk', 'rep')), may hold values from -6 to 6
- degrees: int32 [65536], P(('blk', 'rep')), may hold values from 4 to 64
- tile_values: bfloat16 [512, 16, 8, 128, 128], P(('blk', 'rep')), may hold values from 0 to 1
- tile_rows: int32 [512, 16, 8], P(('blk', 'rep')), may hold values from 0 to 7, as said below
- tile_counts: int32 [512, 16], P(('blk', 'rep')), may hold values from 1 to 8, as said below
- weight: bfloat16 [256, 256], replicated, may hold values from -0.375 to 0.375
- cotangent: bfloat16 [65536, 256], P(('blk', 'rep')), may hold values from -6 to 6
Outputs:
- activations: bfloat16 [65536, 256], P(('blk', 'rep'))
- grad_weight: float32 [256, 256], replicated
- grad_features: bfloat16 [65536, 256], P(('blk', 'rep'))
The draws below stay inside these ranges and needn't reach their ends.
Inputs may be any that keep to these rules, and one draw needn't show every extreme that they name: `tile_rows`: the 8 slots of one owner and distance name the 8 row blocks of its slab, each once. Only the first tile_counts[o, s] slots of owner o and distance s are live. In every draw some slab has all 8 slots live at every distance for every owner in it.
All inputs are finite; a program needn't handle non-finite values.
Results may differ from the reference program's by a relative error of at most 0.0077.
Values may be sent and summed in bfloat16 or wider, within the bound.
No kernel may reach another device: no remote copies, remote signals or barrier semaphores. Data moves between devices by JAX's collectives and lax.ppermute only.
A program may use at most 64 MiB of HBM per device.

```python
import math
import jax
import jax.numpy as jnp
from jax import lax

F = 256
BS = 128
ROWS_DEV = 128
SPAN = 16
CAP = 8
NODES = 65536
N_BLK = 64
N_REP = 8


def draw_tile_rows(key, part):
    scores = jax.random.randint(key, (N_BLK * N_REP, SPAN, CAP), 0, 2 ** 20)
    scores = scores * CAP + jnp.arange(CAP, dtype=jnp.int32)
    return jnp.argsort(scores, axis=-1, stable=True).astype(jnp.int32)


def draw_tile_counts(key, part):
    heavy_key = jax.random.fold_in(key, 11)
    pick_key = jax.random.fold_in(key, 12)
    light_key = jax.random.fold_in(key, 13)
    heavy_set = jax.random.randint(heavy_key, (N_BLK,), 0, 8) == 0
    chosen = jax.random.randint(pick_key, (), 0, N_BLK)
    heavy_set = heavy_set | (jnp.arange(N_BLK) == chosen)
    light_counts = jax.random.randint(light_key, (N_BLK * N_REP, SPAN), 1, CAP // 4 + 2)
    owner_index = jnp.arange(N_BLK * N_REP) // N_REP
    return jnp.where(heavy_set[owner_index][:, None], CAP, light_counts).astype(jnp.int32)


def with_ends(entries, own_key, low, largest):
    longest = entries.shape.index(max(entries.shape))
    spots = []
    for shift in (0, 1):
        where = [jax.random.randint(jax.random.fold_in(own_key, axis), (), 0, length) for axis, length in enumerate(entries.shape)]
        where[longest] = (where[longest] + shift) % entries.shape[longest]
        spots.append(tuple(where))
    return entries.at[spots[0]].set(low).at[spots[1]].set(largest)


def block_levels(key, dims, shards, least, top_value):
    gain, own = 1.0, jax.random.fold_in(key, 6)
    for dim, blocks in shards:
        draws = jnp.exp(jax.random.uniform(jax.random.fold_in(own, dim), (blocks,), jnp.float32, least / len(shards), top_value / len(shards)))
        gain = gain * jnp.repeat(draws, dims[dim] // blocks).reshape([-1 if axis == dim else 1 for axis in range(len(dims))])
    return gain


def normal_values(stream_key, dims, deviation, reach, split=(), held_as=jnp.bfloat16):
    gain = block_levels(stream_key, dims, split, -0.22, 0.18) if split else 1.0
    drawn = jax.random.normal(stream_key, dims, jnp.float32) * deviation * gain
    return jnp.minimum(jnp.maximum(drawn, -reach), reach).astype(held_as)


def setup_inputs(seed: int = 0) -> dict:
    seeds = jax.random.split(jax.random.key(seed), 8)
    features = normal_values(seeds[0], (NODES, F), 1.0, 6.0, ((0, 512),))
    degrees = with_ends(jax.random.randint(seeds[1], (NODES,), 4, 65), jax.random.fold_in(seeds[1], 1), 4, 64).astype(jnp.int32)
    tile_values = jnp.clip(1.0 * jax.random.uniform(seeds[2], (N_BLK * N_REP, SPAN, CAP, BS, ROWS_DEV), jnp.float32) ** block_levels(seeds[2], (N_BLK * N_REP, SPAN, CAP, BS, ROWS_DEV), ((0, 512),), -0.2, 0.2), 0.0, 1.0).astype(jnp.bfloat16)
    tile_rows = draw_tile_rows(jax.random.fold_in(seeds[7], 71), 0)
    tile_counts = draw_tile_counts(jax.random.fold_in(seeds[7], 71), 0)
    weight = normal_values(seeds[5], (F, F), F ** -0.5, 0.375)
    cotangent = normal_values(seeds[6], (NODES, F), 1.0, 6.0, ((0, 512),))
    return {"features": features, "degrees": degrees, "tile_values": tile_values, "tile_rows": tile_rows, "tile_counts": tile_counts, "weight": weight, "cotangent": cotangent}


def reference(features, degrees, tile_values, tile_rows, tile_counts, weight, cotangent):
    inv_root = lax.rsqrt(degrees.astype(jnp.float32))[:, None]
    scaled = (features.astype(jnp.float32) * inv_root).astype(jnp.bfloat16)
    source_view = scaled.reshape(N_BLK, N_REP, ROWS_DEV, F).astype(jnp.float32)
    tile_view = tile_values.reshape(N_BLK, N_REP, SPAN, CAP, BS, ROWS_DEV)
    slot_ids = jnp.arange(CAP, dtype=jnp.int32)
    live_slots = (slot_ids[None, None, :] < tile_counts[:, :, None]).astype(jnp.float32)
    placement = (tile_rows[:, :, :, None] == slot_ids[None, None, None, :]).astype(jnp.float32) * live_slots[:, :, :, None]
    place_view = placement.reshape(N_BLK, N_REP, SPAN, CAP, CAP)
    distances = jnp.arange(SPAN, dtype=jnp.int32)

    def placed_tiles(distance):
        tile_now = lax.dynamic_index_in_dim(tile_view, distance, 2, keepdims=False).astype(jnp.float32)
        place_now = lax.dynamic_index_in_dim(place_view, distance, 2, keepdims=False)
        return jnp.einsum('brkm,brkij->brmij', place_now, tile_now, precision=lax.Precision.HIGHEST)

    def forward_step(total, distance):
        moved = jnp.roll(source_view, distance, axis=0)
        placed = placed_tiles(distance)
        return (total + jnp.einsum('brmij,brjf->brmif', placed, moved, precision=lax.Precision.HIGHEST), None)
    zero_total = jnp.zeros((N_BLK, N_REP, CAP, BS, F), jnp.float32)
    partial_sum, _ = lax.scan(forward_step, zero_total, distances)
    summed = lax.optimization_barrier(jnp.sum(partial_sum, axis=1)).reshape(NODES, F)
    aggregated = (summed * inv_root).astype(jnp.bfloat16)
    pre_act = jnp.dot(aggregated, weight, preferred_element_type=jnp.float32)
    sigma = jax.nn.sigmoid(pre_act)
    activations = (pre_act * sigma).astype(jnp.bfloat16)
    act_grad = (cotangent.astype(jnp.float32) * sigma * (1.0 + pre_act * (1.0 - sigma))).astype(jnp.bfloat16)
    local_weight = lax.dot_general(aggregated, act_grad, (((0,), (0,)), ((), ())), preferred_element_type=jnp.float32)
    grad_weight = local_weight / math.sqrt(NODES)
    back_grad = lax.dot_general(act_grad, weight, (((1,), (1,)), ((), ())), preferred_element_type=jnp.float32)
    back_scaled = (back_grad * inv_root).astype(jnp.bfloat16)
    slab_view = back_scaled.reshape(N_BLK, CAP, BS, F).astype(jnp.float32)

    def backward_step(total, distance):
        placed = placed_tiles(distance)
        local_part = jnp.einsum('brmij,bmif->brjf', placed, slab_view, precision=lax.Precision.HIGHEST)
        return (total + jnp.roll(local_part, -distance, axis=0), None)
    zero_back = jnp.zeros((N_BLK, N_REP, ROWS_DEV, F), jnp.float32)
    back_total, _ = lax.scan(backward_step, zero_back, distances)
    grad_features = (back_total.reshape(NODES, F) * inv_root).astype(jnp.bfloat16)
    return (activations, grad_weight, grad_features)
```

```python
import math

import jax
import jax.numpy as jnp
from jax import lax
from jax.experimental import pallas as pl
from jax.experimental.pallas import tpu as pltpu
from jax.sharding import Mesh, PartitionSpec as P

BF = jnp.bfloat16
F32 = jnp.float32
ROW, COL, REP = "y", ("x", "zl"), ("zh", "core")
N_ROW, N_COL, N_ZH, N_CORE = 8, 8, 4, 2
N_REP = N_ZH * N_CORE


def arrange_kernel(rows_ref, counts_ref, col_ref, tile_ref, out_ref):
    distance = pl.program_id(0)
    col = col_ref[0]
    block = tile_ref.shape[-1]
    live_count = counts_ref[0, distance]
    wrapped = lax.rem(distance, N_COL)
    same_turn = col >= wrapped
    source = jnp.where(same_turn, col - wrapped, col - wrapped + N_COL)
    near = distance < N_COL
    slot = jnp.where(same_turn == near, 1, 0)
    place = source * 2 + slot
    for k in range(tile_ref.shape[2]):
        owner = rows_ref[0, distance, k]
        row = lax.rem(owner, N_CORE) * N_ZH + lax.div(owner, N_CORE)
        tile = tile_ref[0, 0, k]
        tile = jnp.where(k < live_count, tile, jnp.zeros_like(tile))
        out_ref[
            pl.ds(pl.multiple_of(row * block, block), block),
            pl.ds(pl.multiple_of(place * block, block), block),
        ] = tile


def arrange(tile_values, tile_rows, tile_counts, col):
    _, span, cap, rows, cols = tile_values.shape
    size = span * cap * rows * cols
    return pl.pallas_call(
        arrange_kernel,
        out_shape=jax.ShapeDtypeStruct((cap * rows, span * cols), BF),
        grid_spec=pltpu.PrefetchScalarGridSpec(
            num_scalar_prefetch=3,
            grid=(span,),
            in_specs=[pl.BlockSpec((1, 1, cap, rows, cols), lambda s, *_: (0, s, 0, 0, 0))],
            out_specs=pl.BlockSpec((cap * rows, span * cols), lambda s, *_: (0, 0)),
        ),
        cost_estimate=pl.CostEstimate(flops=size, bytes_accessed=4 * size, transcendentals=0),
        name="arrange_tiles",
    )(tile_rows, tile_counts, col, tile_values)


def shifted(block, distance):
    return lax.ppermute(block, ROW, [((i - distance) % N_ROW, i) for i in range(N_ROW)])


def copies_to(block, axis, count):
    return lax.all_to_all(jnp.broadcast_to(block[None], (count,) + block.shape), axis, 0, 0)


def summed_in_f32(stack):
    return jnp.sum(stack.astype(F32), axis=0)


def per_device(features, degrees, tile_values, tile_rows, tile_counts, weight, cotangent):
    own_rows, width = features.shape
    col = lax.axis_index(COL)
    columns = jnp.arange(N_COL, dtype=jnp.int32)[:, None, None]
    inv_root = lax.rsqrt(degrees.astype(F32))[:, None]
    scaled = (features.astype(F32) * inv_root).astype(BF)

    one_back = shifted(scaled, 1)
    two_back = shifted(scaled, 2)
    adjacency = arrange(tile_values, tile_rows, tile_counts, col[None])
    own_or_two = jnp.where(columns >= col, scaled[None], two_back[None])
    offer = jnp.stack([jnp.broadcast_to(one_back[None], own_or_two.shape), own_or_two], axis=1)
    window = lax.all_to_all(offer, COL, 0, 0).reshape(-1, width)

    partial = jnp.dot(adjacency, window, preferred_element_type=F32).astype(BF)
    halves = lax.all_to_all(partial.reshape(N_CORE, -1, width), "core", 0, 0)
    half = summed_in_f32(halves).astype(BF)
    shares = lax.all_to_all(half.reshape(N_ZH, own_rows, width), "zh", 0, 0)
    own_sum = summed_in_f32(shares)

    aggregated = (own_sum * inv_root).astype(BF)
    pre_act = jnp.dot(aggregated, weight, preferred_element_type=F32)
    sigma = jax.nn.sigmoid(pre_act)
    activations = (pre_act * sigma).astype(BF)
    act_grad = (cotangent.astype(F32) * sigma * (1.0 + pre_act * (1.0 - sigma))).astype(BF)
    back_grad = lax.dot_general(
        act_grad, weight, (((1,), (1,)), ((), ())), preferred_element_type=F32
    )
    back_scaled = (back_grad * inv_root).astype(BF)
    along_zh = copies_to(back_scaled, "zh", N_ZH).reshape(-1, width)
    slab_grads = lax.all_gather(along_zh, "core", axis=0, tiled=True)

    local_weight = lax.dot_general(
        aggregated, act_grad, (((0,), (0,)), ((), ())), preferred_element_type=F32
    )
    weight_rows = lax.all_to_all(local_weight.astype(BF).reshape(N_REP, -1, width), REP, 0, 0)
    weight_rows = summed_in_f32(weight_rows).astype(BF)
    weight_rows = summed_in_f32(copies_to(weight_rows, COL, N_COL)).astype(BF)
    weight_rows = summed_in_f32(copies_to(weight_rows, ROW, N_ROW))
    node_total = own_rows * N_ROW * N_COL * N_REP
    weight_rows = (weight_rows / math.sqrt(node_total)).astype(BF)
    grad_weight = copies_to(weight_rows, REP, N_REP).reshape(-1, width).astype(F32)

    returned = lax.dot_general(
        adjacency, slab_grads, (((0,), (0,)), ((), ())), preferred_element_type=F32
    ).astype(BF)
    arrived = lax.all_to_all(
        returned.reshape(N_COL, 2, own_rows, width), COL, 0, 0
    ).astype(F32)
    for_one = jnp.sum(arrived[:, 0], axis=0).astype(BF)
    for_two = jnp.sum(jnp.where(columns < col, arrived[:, 1], 0.0), axis=0).astype(BF)
    for_own = jnp.sum(jnp.where(columns >= col, arrived[:, 1], 0.0), axis=0)
    from_one = shifted(for_one, -1)
    from_two = shifted(for_two, -2)
    back_total = for_own + from_one.astype(F32) + from_two.astype(F32)
    grad_features = (back_total * inv_root).astype(BF)
    return (activations, grad_weight, grad_features)


def solution(mesh):
    fine = Mesh(
        mesh.devices.reshape(N_ROW, 4, 2, N_ZH, N_CORE), ("y", "x", "zl", "zh", "core")
    )
    nodes = ("y", "x", "zl", "zh", "core")
    placed = (
        P(nodes, None),
        P(nodes),
        P(nodes, None, None, None, None),
        P(nodes, None, None),
        P(nodes, None),
        P(),
        P(nodes, None),
    )
    return jax.shard_map(
        per_device,
        mesh=fine,
        in_specs=placed,
        out_specs=(P(nodes, None), P(), P(nodes, None)),
        check_vma=False,
    )
```

```python
import math

import jax
import jax.numpy as jnp
from jax import lax
from jax.experimental import pallas as pl
from jax.experimental.pallas import tpu as pltpu
from jax.sharding import Mesh, PartitionSpec as P


BF = jnp.bfloat16
F32 = jnp.float32
ROW, COL, REP = "y", ("x", "zl"), ("zh", "core")
N_ROW, N_COL, N_ZH, N_CORE = 8, 8, 4, 2
N_REP = N_ZH * N_CORE


def arrange_kernel(rows_ref, counts_ref, col_ref, tile_hbm, out_ref, flip_ref, tiles, arrived):
    _, span, cap, block, _ = tile_hbm.shape

    def fetch(distance):
        return pltpu.make_async_copy(
            tile_hbm.at[0, distance], tiles.at[distance], arrived.at[distance]
        )

    for distance in range(span):
        fetch(distance).start()
    col = col_ref[0]

    def place_distance(distance, carry):
        fetch(distance).wait()
        live_count = counts_ref[0, distance]
        wrapped = lax.rem(distance, N_COL)
        same_turn = col >= wrapped
        source = jnp.where(same_turn, col - wrapped, col - wrapped + N_COL)
        near = distance < N_COL
        slot = jnp.where(same_turn == near, 1, 0)
        at_col = pl.ds(pl.multiple_of((source * 2 + slot) * block, block), block)
        for k in range(cap):
            owner = rows_ref[0, distance, k]
            row = lax.rem(owner, N_CORE) * N_ZH + lax.div(owner, N_CORE)
            at_row = pl.ds(pl.multiple_of(row * block, block), block)
            tile = tiles[distance, k]
            tile = jnp.where(k < live_count, tile, jnp.zeros_like(tile))
            out_ref[at_row, at_col] = tile
            flip_ref[at_col, at_row] = tile.T
        return carry

    lax.fori_loop(0, span, place_distance, 0)


def arrange(tile_values, tile_rows, tile_counts, col):
    _, span, cap, rows, cols = tile_values.shape
    size = span * cap * rows * cols
    whole = pl.BlockSpec(memory_space=pltpu.VMEM)
    scalars = pl.BlockSpec(memory_space=pltpu.SMEM)
    return pl.pallas_call(
        arrange_kernel,
        out_shape=(
            jax.ShapeDtypeStruct((cap * rows, span * cols), BF),
            jax.ShapeDtypeStruct((span * cols, cap * rows), BF),
        ),
        in_specs=[scalars, scalars, scalars, pl.BlockSpec(memory_space=pltpu.HBM)],
        out_specs=(whole, whole),
        scratch_shapes=[
            pltpu.VMEM((span, cap, rows, cols), BF),
            pltpu.SemaphoreType.DMA((span,)),
        ],
        cost_estimate=pl.CostEstimate(flops=size, bytes_accessed=4 * size, transcendentals=0),
        name="arrange_tiles",
    )(tile_rows, tile_counts, col, tile_values)


def shifted(block, distance):
    return lax.ppermute(block, ROW, [((i - distance) % N_ROW, i) for i in range(N_ROW)])


def copies_to(block, axis, count):
    return lax.all_to_all(jnp.broadcast_to(block[None], (count,) + block.shape), axis, 0, 0)


def summed_in_f32(blocks):
    total = blocks[0].astype(F32)
    for block in blocks[1:]:
        total = total + block.astype(F32)
    return total


def per_device(features, degrees, tile_values, tile_rows, tile_counts, weight, cotangent):
    own_rows, width = features.shape
    col = lax.axis_index(COL)
    columns = jnp.arange(N_COL, dtype=jnp.int32)[:, None, None]
    inv_root = lax.rsqrt(degrees.astype(F32))[:, None]
    scaled = (features.astype(F32) * inv_root).astype(BF)

    one_back = shifted(scaled, 1)
    two_back = shifted(scaled, 2)
    adjacency, flipped = arrange(tile_values, tile_rows, tile_counts, col[None])
    own_or_two = jnp.where(columns >= col, scaled[None], two_back[None])
    offer = jnp.stack([jnp.broadcast_to(one_back[None], own_or_two.shape), own_or_two], axis=1)
    window = lax.all_to_all(offer, COL, 0, 0).reshape(-1, width)

    partial = jnp.dot(adjacency, window, preferred_element_type=F32).astype(BF)
    core = lax.axis_index("core")
    halves = lax.all_to_all(partial.reshape(N_CORE, -1, width), "core", 0, 0)
    half = summed_in_f32(halves).astype(BF)
    shares = lax.all_to_all(half.reshape(N_ZH, own_rows, width), "zh", 0, 0)
    own_sum = summed_in_f32(shares)

    aggregated = (own_sum * inv_root).astype(BF)
    pre_act = jnp.dot(aggregated, weight, preferred_element_type=F32)
    sigma = jax.nn.sigmoid(pre_act)
    activations = (pre_act * sigma).astype(BF)
    act_grad = (cotangent.astype(F32) * sigma * (1.0 + pre_act * (1.0 - sigma))).astype(BF)
    back_grad = lax.dot_general(
        act_grad, weight, (((1,), (1,)), ((), ())), preferred_element_type=F32
    )
    back_scaled = (back_grad * inv_root).astype(BF)
    local_weight = lax.dot_general(
        aggregated, act_grad, (((0,), (0,)), ((), ())), preferred_element_type=F32
    ).astype(BF)
    copies = jnp.broadcast_to(back_scaled[None], (N_ZH,) + back_scaled.shape)
    offer = jnp.concatenate([copies, local_weight.reshape(N_ZH, -1, width)], axis=1)
    given = lax.all_to_all(offer, "zh", 0, 0)
    along_zh = given[:, :own_rows].reshape(-1, width)
    weight_part = summed_in_f32(given[:, own_rows:]).astype(BF)
    pair = lax.all_gather(
        jnp.concatenate([along_zh, weight_part], axis=0), "core", axis=0, tiled=False
    )
    gathered = along_zh.shape[0]
    slab_grads = pair[:, :gathered].reshape(-1, width)
    weight_pair = pair[:, gathered:].reshape(N_CORE, N_CORE, -1, width)
    weight_rows = summed_in_f32(lax.dynamic_index_in_dim(weight_pair, core, 1, keepdims=False))

    along_y = copies_to(weight_rows.astype(BF), ROW, N_ROW)
    weight_rows = summed_in_f32(along_y).astype(BF)
    returned = jnp.dot(flipped, slab_grads, preferred_element_type=F32).astype(BF)
    returned = returned.reshape(N_COL, 2 * own_rows, width)
    copies = jnp.broadcast_to(weight_rows[None], (N_COL,) + weight_rows.shape)
    home = lax.all_to_all(jnp.concatenate([returned, copies], axis=1), COL, 0, 0)
    node_total = own_rows * N_ROW * N_COL * N_REP
    weight_rows = (summed_in_f32(home[:, 2 * own_rows :]) / math.sqrt(node_total)).astype(BF)
    along_rep = copies_to(weight_rows, REP, N_REP)
    grad_weight = along_rep.reshape(-1, width).astype(F32)

    arrived = home[:, : 2 * own_rows].reshape(N_COL, 2, own_rows, width)
    for_one = summed_in_f32(arrived[:, 0]).astype(BF)
    nothing = jnp.zeros((), BF)
    for_two = summed_in_f32(jnp.where(columns < col, arrived[:, 1], nothing)).astype(BF)
    for_own = summed_in_f32(jnp.where(columns >= col, arrived[:, 1], nothing))
    from_two = shifted(for_two, -2)
    from_one = shifted(for_one, -1)
    back_total = for_own + from_one.astype(F32) + from_two.astype(F32)
    grad_features = (back_total * inv_root).astype(BF)
    return (activations, grad_weight, grad_features)


def solution(mesh):
    fine = Mesh(
        mesh.devices.reshape(N_ROW, 4, 2, N_ZH, N_CORE), ("y", "x", "zl", "zh", "core")
    )
    nodes = ("y", "x", "zl", "zh", "core")
    placed = (
        P(nodes, None),
        P(nodes),
        P(nodes, None, None, None, None),
        P(nodes, None, None),
        P(nodes, None),
        P(),
        P(nodes, None),
    )

    return jax.shard_map(
        per_device,
        mesh=fine,
        in_specs=placed,
        out_specs=(P(nodes, None), P(), P(nodes, None)),
        check_vma=False,
    )
```

```python
import math

import jax
import jax.numpy as jnp
from jax import lax
from jax.experimental import pallas as pl
from jax.experimental.pallas import tpu as pltpu
from jax.sharding import Mesh, PartitionSpec as P


BF = jnp.bfloat16
F32 = jnp.float32
ROW, COL, REP = "y", ("x", "zl"), ("zh", "core")
N_ROW, N_COL, N_ZH, N_CORE = 8, 8, 4, 2
N_REP = N_ZH * N_CORE
DEGREE_ROWS = 16


def arrange_kernel(rows_ref, counts_ref, here_ref, tile_hbm, out_ref, flip_ref, tiles, arrived):
    _, span, cap, block, _ = tile_hbm.shape

    def fetch(distance):
        return pltpu.make_async_copy(
            tile_hbm.at[0, distance], tiles.at[distance], arrived.at[distance]
        )

    for distance in range(span):
        fetch(distance).start()
    col, core = here_ref[0], here_ref[1]

    def place_distance(distance, carry):
        fetch(distance).wait()
        live_count = counts_ref[0, distance]
        wrapped = lax.rem(distance, N_COL)
        same_turn = col >= wrapped
        source = jnp.where(same_turn, col - wrapped, col - wrapped + N_COL)
        near = distance < N_COL
        slot = jnp.where(same_turn == near, 1, 0)
        at_col = pl.ds(pl.multiple_of((source * 2 + slot) * block, block), block)
        for k in range(cap):
            owner = rows_ref[0, distance, k]
            owner_core, owner_zh = lax.rem(owner, N_CORE), lax.div(owner, N_CORE)
            far = jnp.where(owner_core == core, 0, N_ZH)
            at_row = pl.ds(pl.multiple_of((far + owner_zh) * block, block), block)
            at_flip = pl.ds(pl.multiple_of((owner_core * N_ZH + owner_zh) * block, block), block)
            tile = tiles[distance, k]
            tile = jnp.where(k < live_count, tile, jnp.zeros_like(tile))
            out_ref[at_row, at_col] = tile
            flip_ref[at_col, at_flip] = tile.T
        return carry

    lax.fori_loop(0, span, place_distance, 0)


def arrange(tile_values, tile_rows, tile_counts, here):
    _, span, cap, rows, cols = tile_values.shape
    size = span * cap * rows * cols
    whole = pl.BlockSpec(memory_space=pltpu.VMEM)
    scalars = pl.BlockSpec(memory_space=pltpu.SMEM)
    return pl.pallas_call(
        arrange_kernel,
        out_shape=(
            jax.ShapeDtypeStruct((cap * rows, span * cols), BF),
            jax.ShapeDtypeStruct((span * cols, cap * rows), BF),
        ),
        in_specs=[scalars, scalars, scalars, pl.BlockSpec(memory_space=pltpu.HBM)],
        out_specs=(whole, whole),
        scratch_shapes=[
            pltpu.VMEM((span, cap, rows, cols), BF),
            pltpu.SemaphoreType.DMA((span,)),
        ],
        cost_estimate=pl.CostEstimate(flops=size, bytes_accessed=4 * size, transcendentals=0),
        name="arrange_tiles",
    )(tile_rows, tile_counts, here, tile_values)


def shifted(block, distance):
    return lax.ppermute(block, ROW, [((i - distance) % N_ROW, i) for i in range(N_ROW)])


def copies_to(block, axis, count):
    return lax.all_to_all(jnp.broadcast_to(block[None], (count,) + block.shape), axis, 0, 0)


def summed_in_f32(blocks):
    total = blocks[0].astype(F32)
    for block in blocks[1:]:
        total = total + block.astype(F32)
    return total


def per_device(features, degrees, tile_values, tile_rows, tile_counts, weight, cotangent):
    own_rows, width = features.shape
    col, core, zh = lax.axis_index(COL), lax.axis_index("core"), lax.axis_index("zh")
    columns = jnp.arange(N_COL, dtype=jnp.int32)[:, None, None]
    inv_root = lax.rsqrt(degrees.astype(F32))[:, None]
    scaled = (features.astype(F32) * inv_root).astype(BF)

    one_back = shifted(scaled, 1)
    two_back = shifted(scaled, 2)
    adjacency, flipped = arrange(
        tile_values, tile_rows, tile_counts, jnp.stack([col, core])
    )
    own_or_two = jnp.where(columns >= col, scaled[None], two_back[None])
    offer = jnp.stack([jnp.broadcast_to(one_back[None], own_or_two.shape), own_or_two], axis=1)
    window = lax.all_to_all(offer, COL, 0, 0).reshape(-1, width)

    partial = jnp.dot(adjacency, window, preferred_element_type=F32)
    kept, sent = jnp.split(partial, 2, axis=0)
    other = lax.ppermute(sent.astype(BF), "core", [(0, 1), (1, 0)])
    half = (kept + other.astype(F32)).astype(BF)
    degree_rows = jnp.zeros((DEGREE_ROWS, width), BF).at[0, :own_rows].set(degrees.astype(BF))
    told = copies_to(jnp.concatenate([half, cotangent, degree_rows], axis=0), "zh", N_ZH)
    zh_rows = N_ZH * own_rows
    zh_sum = summed_in_f32(told[:, :zh_rows])
    zh_cotangent = told[:, zh_rows : zh_rows + own_rows].reshape(zh_rows, width)
    zh_degrees = told[:, zh_rows + own_rows, :own_rows].reshape(zh_rows)
    zh_inv_root = lax.rsqrt(zh_degrees.astype(F32))[:, None]

    aggregated = (zh_sum * zh_inv_root).astype(BF)
    pre_act = jnp.dot(aggregated, weight, preferred_element_type=F32)
    sigma = jax.nn.sigmoid(pre_act)
    activations = lax.dynamic_slice_in_dim((pre_act * sigma).astype(BF), zh * own_rows, own_rows)
    act_grad = (zh_cotangent.astype(F32) * sigma * (1.0 + pre_act * (1.0 - sigma))).astype(BF)
    zh_weight = lax.dot_general(
        aggregated, act_grad, (((0,), (0,)), ((), ())), preferred_element_type=F32
    )
    back_grad = lax.dot_general(
        act_grad, weight, (((1,), (1,)), ((), ())), preferred_element_type=F32
    )
    back_scaled = (back_grad * zh_inv_root).astype(BF)
    slab_grads = lax.all_gather(back_scaled, "core", axis=0, tiled=True)
    share = width // N_ZH
    weight_rows = lax.dynamic_slice_in_dim(zh_weight, zh * share, share)

    along_y = copies_to(weight_rows.astype(BF), ROW, N_ROW)
    weight_rows = summed_in_f32(along_y).astype(BF)
    returned = jnp.dot(flipped, slab_grads, preferred_element_type=F32).astype(BF)
    returned = returned.reshape(N_COL, 2 * own_rows, width)
    copies = jnp.broadcast_to(weight_rows[None], (N_COL,) + weight_rows.shape)
    home = lax.all_to_all(jnp.concatenate([returned, copies], axis=1), COL, 0, 0)
    node_total = own_rows * N_ROW * N_COL * N_REP
    weight_rows = (summed_in_f32(home[:, 2 * own_rows :]) / math.sqrt(node_total)).astype(BF)
    along_rep = copies_to(weight_rows, REP, N_REP)
    along_rep = along_rep.reshape(N_ZH, N_CORE, share, width).astype(F32)
    grad_weight = (along_rep[:, 0] + along_rep[:, 1]).reshape(-1, width)

    arrived = home[:, : 2 * own_rows].reshape(N_COL, 2, own_rows, width)
    for_one = summed_in_f32(arrived[:, 0]).astype(BF)
    nothing = jnp.zeros((), BF)
    for_two = summed_in_f32(jnp.where(columns < col, arrived[:, 1], nothing)).astype(BF)
    for_own = summed_in_f32(jnp.where(columns >= col, arrived[:, 1], nothing))
    from_two = shifted(for_two, -2)
    from_one = shifted(for_one, -1)
    back_total = for_own + from_one.astype(F32) + from_two.astype(F32)
    grad_features = (back_total * inv_root).astype(BF)
    return (activations, grad_weight, grad_features)


def solution(mesh):
    fine = Mesh(
        mesh.devices.reshape(N_ROW, 4, 2, N_ZH, N_CORE), ("y", "x", "zl", "zh", "core")
    )
    nodes = ("y", "x", "zl", "zh", "core")
    placed = (
        P(nodes, None),
        P(nodes),
        P(nodes, None, None, None, None),
        P(nodes, None, None),
        P(nodes, None),
        P(),
        P(nodes, None),
    )

    return jax.shard_map(
        per_device,
        mesh=fine,
        in_specs=placed,
        out_specs=(P(nodes, None), P(), P(nodes, None)),
        check_vma=False,
    )
```

```python
import math

import jax
import jax.numpy as jnp
from jax import lax
from jax.experimental import pallas as pl
from jax.experimental.pallas import tpu as pltpu
from jax.sharding import Mesh, PartitionSpec as P


BF = jnp.bfloat16
F32 = jnp.float32
ROW, COL, REP = "y", ("x", "zl"), ("zh", "core")
N_ROW, N_COL, N_ZH, N_CORE = 8, 8, 4, 2
N_REP = N_ZH * N_CORE


def arrange_kernel(rows_ref, counts_ref, here_ref, tile_hbm, out_ref, flip_ref, tiles, arrived):
    _, span, cap, block, _ = tile_hbm.shape

    def fetch(distance):
        return pltpu.make_async_copy(
            tile_hbm.at[0, distance], tiles.at[distance], arrived.at[distance]
        )

    for distance in range(span):
        fetch(distance).start()
    col, core = here_ref[0], here_ref[1]

    def place_distance(distance, carry):
        fetch(distance).wait()
        live_count = counts_ref[0, distance]
        wrapped = lax.rem(distance, N_COL)
        same_turn = col >= wrapped
        source = jnp.where(same_turn, col - wrapped, col - wrapped + N_COL)
        near = distance < N_COL
        slot = jnp.where(same_turn == near, 1, 0)
        at_col = pl.ds(pl.multiple_of((source * 2 + slot) * block, block), block)
        for k in range(cap):
            owner = rows_ref[0, distance, k]
            owner_core, owner_zh = lax.rem(owner, N_CORE), lax.div(owner, N_CORE)
            far = jnp.where(owner_core == core, 0, N_ZH)
            at_row = pl.ds(pl.multiple_of((far + owner_zh) * block, block), block)
            at_flip = pl.ds(pl.multiple_of((owner_core * N_ZH + owner_zh) * block, block), block)
            tile = tiles[distance, k]
            tile = jnp.where(k < live_count, tile, jnp.zeros_like(tile))
            out_ref[at_row, at_col] = tile
            flip_ref[at_col, at_flip] = tile.T
        return carry

    lax.fori_loop(0, span, place_distance, 0)


def arrange(tile_values, tile_rows, tile_counts, here):
    _, span, cap, rows, cols = tile_values.shape
    size = span * cap * rows * cols
    whole = pl.BlockSpec(memory_space=pltpu.VMEM)
    scalars = pl.BlockSpec(memory_space=pltpu.SMEM)
    return pl.pallas_call(
        arrange_kernel,
        out_shape=(
            jax.ShapeDtypeStruct((cap * rows, span * cols), BF),
            jax.ShapeDtypeStruct((span * cols, cap * rows), BF),
        ),
        in_specs=[scalars, scalars, scalars, pl.BlockSpec(memory_space=pltpu.HBM)],
        out_specs=(whole, whole),
        scratch_shapes=[
            pltpu.VMEM((span, cap, rows, cols), BF),
            pltpu.SemaphoreType.DMA((span,)),
        ],
        cost_estimate=pl.CostEstimate(flops=size, bytes_accessed=4 * size, transcendentals=0),
        name="arrange_tiles",
    )(tile_rows, tile_counts, here, tile_values)


def shifted(block, distance):
    return lax.ppermute(block, ROW, [((i - distance) % N_ROW, i) for i in range(N_ROW)])


def copies_to(block, axis, count):
    return lax.all_to_all(jnp.broadcast_to(block[None], (count,) + block.shape), axis, 0, 0)


def summed_in_f32(blocks):
    total = blocks[0].astype(F32)
    for block in blocks[1:]:
        total = total + block.astype(F32)
    return total


def per_device(features, degrees, tile_values, tile_rows, tile_counts, weight, cotangent):
    own_rows, width = features.shape
    col, core = lax.axis_index(COL), lax.axis_index("core")
    columns = jnp.arange(N_COL, dtype=jnp.int32)[:, None, None]
    inv_root = lax.rsqrt(degrees.astype(F32))[:, None]
    scaled = (features.astype(F32) * inv_root).astype(BF)

    one_back = shifted(scaled, 1)
    two_back = shifted(scaled, 2)
    adjacency, flipped = arrange(
        tile_values, tile_rows, tile_counts, jnp.stack([col, core])
    )
    own_or_two = jnp.where(columns >= col, scaled[None], two_back[None])
    offer = jnp.stack([jnp.broadcast_to(one_back[None], own_or_two.shape), own_or_two], axis=1)
    window = lax.all_to_all(offer, COL, 0, 0).reshape(-1, width)

    partial = jnp.dot(adjacency, window, preferred_element_type=F32)
    kept, sent = jnp.split(partial, 2, axis=0)
    other = lax.ppermute(sent.astype(BF), "core", [(0, 1), (1, 0)])
    half = (kept + other.astype(F32)).astype(BF)
    shares = lax.all_to_all(half.reshape(N_ZH, own_rows, width), "zh", 0, 0)
    own_sum = summed_in_f32(shares)

    aggregated = (own_sum * inv_root).astype(BF)
    pre_act = jnp.dot(aggregated, weight, preferred_element_type=F32)
    sigma = jax.nn.sigmoid(pre_act)
    activations = (pre_act * sigma).astype(BF)
    act_grad = (cotangent.astype(F32) * sigma * (1.0 + pre_act * (1.0 - sigma))).astype(BF)
    back_grad = lax.dot_general(
        act_grad, weight, (((1,), (1,)), ((), ())), preferred_element_type=F32
    )
    back_scaled = (back_grad * inv_root).astype(BF)
    local_weight = lax.dot_general(
        aggregated, act_grad, (((0,), (0,)), ((), ())), preferred_element_type=F32
    ).astype(BF)
    copies = jnp.broadcast_to(back_scaled[None], (N_ZH,) + back_scaled.shape)
    offer = jnp.concatenate([copies, local_weight.reshape(N_ZH, -1, width)], axis=1)
    given = lax.all_to_all(offer, "zh", 0, 0)
    along_zh = given[:, :own_rows].reshape(-1, width)
    weight_rows = summed_in_f32(given[:, own_rows:])
    share = weight_rows.shape[0]
    slab_grads = lax.all_gather(along_zh, "core", axis=0, tiled=True)

    along_y = copies_to(weight_rows.astype(BF), ROW, N_ROW)
    weight_rows = summed_in_f32(along_y).astype(BF)
    returned = jnp.dot(flipped, slab_grads, preferred_element_type=F32).astype(BF)
    returned = returned.reshape(N_COL, 2 * own_rows, width)
    copies = jnp.broadcast_to(weight_rows[None], (N_COL,) + weight_rows.shape)
    home = lax.all_to_all(jnp.concatenate([returned, copies], axis=1), COL, 0, 0)
    node_total = own_rows * N_ROW * N_COL * N_REP
    weight_rows = (summed_in_f32(home[:, 2 * own_rows :]) / math.sqrt(node_total)).astype(BF)
    along_rep = copies_to(weight_rows, REP, N_REP)
    along_rep = along_rep.reshape(N_ZH, N_CORE, share, width).astype(F32)
    grad_weight = (along_rep[:, 0] + along_rep[:, 1]).reshape(-1, width)

    arrived = home[:, : 2 * own_rows].reshape(N_COL, 2, own_rows, width)
    for_one = summed_in_f32(arrived[:, 0]).astype(BF)
    nothing = jnp.zeros((), BF)
    for_two = summed_in_f32(jnp.where(columns < col, arrived[:, 1], nothing)).astype(BF)
    for_own = summed_in_f32(jnp.where(columns >= col, arrived[:, 1], nothing))
    from_two = shifted(for_two, -2)
    from_one = shifted(for_one, -1)
    back_total = for_own + from_one.astype(F32) + from_two.astype(F32)
    grad_features = (back_total * inv_root).astype(BF)
    return (activations, grad_weight, grad_features)


def solution(mesh):
    fine = Mesh(
        mesh.devices.reshape(N_ROW, 4, 2, N_ZH, N_CORE), ("y", "x", "zl", "zh", "core")
    )
    nodes = ("y", "x", "zl", "zh", "core")
    placed = (
        P(nodes, None),
        P(nodes),
        P(nodes, None, None, None, None),
        P(nodes, None, None),
        P(nodes, None),
        P(),
        P(nodes, None),
    )

    return jax.shard_map(
        per_device,
        mesh=fine,
        in_specs=placed,
        out_specs=(P(nodes, None), P(), P(nodes, None)),
        check_vma=False,
    )
```

```python
import math

import jax
import jax.numpy as jnp
from jax import lax
from jax.experimental import pallas as pl
from jax.experimental.pallas import tpu as pltpu
from jax.sharding import Mesh, PartitionSpec as P


BF = jnp.bfloat16
F32 = jnp.float32
PAIR, GROUP, REP = "yp", ("ye", "x", "zl"), ("zh", "core")
N_PAIR, N_GROUP, N_ZH, N_CORE = 4, 16, 4, 2
N_REP = N_ZH * N_CORE


def arrange_kernel(rows_ref, counts_ref, here_ref, tile_hbm, out_ref, flip_ref, tiles, arrived):
    _, span, cap, block, _ = tile_hbm.shape

    def fetch(distance):
        return pltpu.make_async_copy(
            tile_hbm.at[0, distance], tiles.at[distance], arrived.at[distance]
        )

    for distance in range(span):
        fetch(distance).start()
    place, core = here_ref[0], here_ref[1]

    def place_distance(distance, carry):
        fetch(distance).wait()
        live_count = counts_ref[0, distance]
        source = lax.rem(place + (span - distance), span)
        at_col = pl.ds(pl.multiple_of(source * block, block), block)
        for k in range(cap):
            owner = rows_ref[0, distance, k]
            owner_core, owner_zh = lax.rem(owner, N_CORE), lax.div(owner, N_CORE)
            far = jnp.where(owner_core == core, 0, N_ZH)
            at_row = pl.ds(pl.multiple_of((far + owner_zh) * block, block), block)
            at_flip = pl.ds(pl.multiple_of((owner_core * N_ZH + owner_zh) * block, block), block)
            tile = tiles[distance, k]
            tile = jnp.where(k < live_count, tile, jnp.zeros_like(tile))
            out_ref[at_row, at_col] = tile
            flip_ref[at_col, at_flip] = tile.T
        return carry

    lax.fori_loop(0, span, place_distance, 0)


def arrange(tile_values, tile_rows, tile_counts, here):
    _, span, cap, rows, cols = tile_values.shape
    size = span * cap * rows * cols
    whole = pl.BlockSpec(memory_space=pltpu.VMEM)
    scalars = pl.BlockSpec(memory_space=pltpu.SMEM)
    return pl.pallas_call(
        arrange_kernel,
        out_shape=(
            jax.ShapeDtypeStruct((cap * rows, span * cols), BF),
            jax.ShapeDtypeStruct((span * cols, cap * rows), BF),
        ),
        in_specs=[scalars, scalars, scalars, pl.BlockSpec(memory_space=pltpu.HBM)],
        out_specs=(whole, whole),
        scratch_shapes=[
            pltpu.VMEM((span, cap, rows, cols), BF),
            pltpu.SemaphoreType.DMA((span,)),
        ],
        cost_estimate=pl.CostEstimate(flops=size, bytes_accessed=4 * size, transcendentals=0),
        name="arrange_tiles",
    )(tile_rows, tile_counts, here, tile_values)


def shifted(block, distance):
    return lax.ppermute(block, PAIR, [((i - distance) % N_PAIR, i) for i in range(N_PAIR)])


def copies_to(block, axis, count):
    return lax.all_to_all(jnp.broadcast_to(block[None], (count,) + block.shape), axis, 0, 0)


def summed_in_f32(blocks):
    total = blocks[0].astype(F32)
    for block in blocks[1:]:
        total = total + block.astype(F32)
    return total


def per_device(features, degrees, tile_values, tile_rows, tile_counts, weight, cotangent):
    own_rows, width = features.shape
    place, core = lax.axis_index(GROUP), lax.axis_index("core")
    places = jnp.arange(N_GROUP, dtype=jnp.int32)[:, None, None]
    inv_root = lax.rsqrt(degrees.astype(F32))[:, None]
    scaled = (features.astype(F32) * inv_root).astype(BF)

    pair_back = shifted(scaled, 1)
    adjacency, flipped = arrange(
        tile_values, tile_rows, tile_counts, jnp.stack([place, core])
    )
    offer = jnp.where(places >= place, scaled[None], pair_back[None])
    window = lax.all_to_all(offer, GROUP, 0, 0).reshape(-1, width)

    partial = jnp.dot(adjacency, window, preferred_element_type=F32)
    kept, sent = jnp.split(partial, 2, axis=0)
    other = lax.ppermute(sent.astype(BF), "core", [(0, 1), (1, 0)])
    half = (kept + other.astype(F32)).astype(BF)
    shares = lax.all_to_all(half.reshape(N_ZH, own_rows, width), "zh", 0, 0)
    own_sum = summed_in_f32(shares)

    aggregated = (own_sum * inv_root).astype(BF)
    pre_act = jnp.dot(aggregated, weight, preferred_element_type=F32)
    sigma = jax.nn.sigmoid(pre_act)
    activations = (pre_act * sigma).astype(BF)
    act_grad = (cotangent.astype(F32) * sigma * (1.0 + pre_act * (1.0 - sigma))).astype(BF)
    back_grad = lax.dot_general(
        act_grad, weight, (((1,), (1,)), ((), ())), preferred_element_type=F32
    )
    back_scaled = (back_grad * inv_root).astype(BF)
    local_weight = lax.dot_general(
        aggregated, act_grad, (((0,), (0,)), ((), ())), preferred_element_type=F32
    ).astype(BF)
    copies = jnp.broadcast_to(back_scaled[None], (N_ZH,) + back_scaled.shape)
    offer = jnp.concatenate([copies, local_weight.reshape(N_ZH, -1, width)], axis=1)
    given = lax.all_to_all(offer, "zh", 0, 0)
    along_zh = given[:, :own_rows].reshape(-1, width)
    weight_rows = summed_in_f32(given[:, own_rows:])
    share = weight_rows.shape[0]
    slab_grads = lax.all_gather(along_zh, "core", axis=0, tiled=True)

    along_y = copies_to(weight_rows.astype(BF), PAIR, N_PAIR)
    weight_rows = summed_in_f32(along_y).astype(BF)
    returned = jnp.dot(flipped, slab_grads, preferred_element_type=F32).astype(BF)
    returned = returned.reshape(N_GROUP, own_rows, width)
    copies = jnp.broadcast_to(weight_rows[None], (N_GROUP,) + weight_rows.shape)
    home = lax.all_to_all(jnp.concatenate([returned, copies], axis=1), GROUP, 0, 0)
    node_total = own_rows * N_PAIR * N_GROUP * N_REP
    weight_rows = (summed_in_f32(home[:, own_rows:]) / math.sqrt(node_total)).astype(BF)
    along_rep = copies_to(weight_rows, REP, N_REP)
    along_rep = along_rep.reshape(N_ZH, N_CORE, share, width).astype(F32)
    grad_weight = (along_rep[:, 0] + along_rep[:, 1]).reshape(-1, width)

    arrived = home[:, :own_rows]
    nothing = jnp.zeros((), BF)
    for_back = summed_in_f32(jnp.where(places < place, arrived, nothing)).astype(BF)
    for_own = summed_in_f32(jnp.where(places >= place, arrived, nothing))
    from_next = shifted(for_back, -1)
    back_total = for_own + from_next.astype(F32)
    grad_features = (back_total * inv_root).astype(BF)
    return (activations, grad_weight, grad_features)


def solution(mesh):
    fine = Mesh(
        mesh.devices.reshape(N_PAIR, 2, 4, 2, N_ZH, N_CORE), (PAIR,) + GROUP + REP
    )
    nodes = (PAIR,) + GROUP + REP
    placed = (
        P(nodes, None),
        P(nodes),
        P(nodes, None, None, None, None),
        P(nodes, None, None),
        P(nodes, None),
        P(),
        P(nodes, None),
    )

    return jax.shard_map(
        per_device,
        mesh=fine,
        in_specs=placed,
        out_specs=(P(nodes, None), P(), P(nodes, None)),
        check_vma=False,
    )
```

```python
import math

import jax
import jax.numpy as jnp
from jax import lax
from jax.experimental import pallas as pl
from jax.experimental.pallas import tpu as pltpu
from jax.sharding import Mesh, PartitionSpec as P


BF = jnp.bfloat16
F32 = jnp.float32
ROW, COL, REP = "y", ("x", "zl"), ("zh", "core")
N_ROW, N_COL, N_ZH, N_CORE = 8, 8, 4, 2
N_REP = N_ZH * N_CORE


def arrange_kernel(rows_ref, counts_ref, here_ref, tile_hbm, out_ref, flip_ref, tiles, arrived):
    _, span, cap, block, _ = tile_hbm.shape

    def fetch(distance):
        return pltpu.make_async_copy(
            tile_hbm.at[0, distance], tiles.at[distance], arrived.at[distance]
        )

    for distance in range(span):
        fetch(distance).start()
    col, core = here_ref[0], here_ref[1]

    def place_distance(distance, carry):
        fetch(distance).wait()
        live_count = counts_ref[0, distance]
        wrapped = lax.rem(distance, N_COL)
        same_turn = col >= wrapped
        source = jnp.where(same_turn, col - wrapped, col - wrapped + N_COL)
        near = distance < N_COL
        slot = jnp.where(same_turn == near, 1, 0)
        at_col = pl.ds(pl.multiple_of((source * 2 + slot) * block, block), block)
        for k in range(cap):
            owner = rows_ref[0, distance, k]
            owner_core, owner_zh = lax.rem(owner, N_CORE), lax.div(owner, N_CORE)
            far = jnp.where(owner_core == core, 0, N_ZH)
            at_row = pl.ds(pl.multiple_of((far + owner_zh) * block, block), block)
            at_flip = pl.ds(pl.multiple_of((owner_core * N_ZH + owner_zh) * block, block), block)
            tile = tiles[distance, k]
            tile = jnp.where(k < live_count, tile, jnp.zeros_like(tile))
            out_ref[at_row, at_col] = tile
            flip_ref[at_col, at_flip] = tile.T
        return carry

    lax.fori_loop(0, span, place_distance, 0)


def arrange(tile_values, tile_rows, tile_counts, here):
    _, span, cap, rows, cols = tile_values.shape
    size = span * cap * rows * cols
    whole = pl.BlockSpec(memory_space=pltpu.VMEM)
    scalars = pl.BlockSpec(memory_space=pltpu.SMEM)
    return pl.pallas_call(
        arrange_kernel,
        out_shape=(
            jax.ShapeDtypeStruct((cap * rows, span * cols), BF),
            jax.ShapeDtypeStruct((span * cols, cap * rows), BF),
        ),
        in_specs=[scalars, scalars, scalars, pl.BlockSpec(memory_space=pltpu.HBM)],
        out_specs=(whole, whole),
        scratch_shapes=[
            pltpu.VMEM((span, cap, rows, cols), BF),
            pltpu.SemaphoreType.DMA((span,)),
        ],
        cost_estimate=pl.CostEstimate(flops=size, bytes_accessed=4 * size, transcendentals=0),
        name="arrange_tiles",
    )(tile_rows, tile_counts, here, tile_values)


def product_kernel(adjacency_hbm, window_ref, kept_ref, sent_ref, blocks, arrived):
    count, step, _ = blocks.shape
    half = kept_ref.shape[0]

    def fetch(index):
        return pltpu.make_async_copy(
            adjacency_hbm.at[pl.ds(index * step, step)], blocks.at[index], arrived.at[index]
        )

    for index in range(count):
        fetch(index).start()
    for index in range(count):
        fetch(index).wait()
        rows = jnp.dot(blocks[index], window_ref[...], preferred_element_type=F32)
        start = index * step
        if start < half:
            kept_ref[start : start + step] = rows
        else:
            sent_ref[start - half : start - half + step] = rows.astype(BF)


def product(adjacency, window):
    rows, depth = adjacency.shape
    width = window.shape[1]
    whole = pl.BlockSpec(memory_space=pltpu.VMEM)
    return pl.pallas_call(
        product_kernel,
        out_shape=(
            pltpu.VMEM((rows // 2, width), F32),
            pltpu.VMEM((rows // 2, width), BF),
        ),
        in_specs=[pl.BlockSpec(memory_space=pltpu.HBM), whole],
        out_specs=(whole, whole),
        scratch_shapes=[
            pltpu.VMEM((N_ZH, rows // N_ZH, depth), BF),
            pltpu.SemaphoreType.DMA((N_ZH,)),
        ],
        cost_estimate=pl.CostEstimate(
            flops=2 * rows * depth * width,
            bytes_accessed=2 * rows * depth,
            transcendentals=0,
        ),
        name="forward_product",
    )(adjacency, window)


def shifted(block, distance):
    return lax.ppermute(block, ROW, [((i - distance) % N_ROW, i) for i in range(N_ROW)])


def copies_to(block, axis, count):
    return lax.all_to_all(jnp.broadcast_to(block[None], (count,) + block.shape), axis, 0, 0)


def summed_in_f32(blocks):
    total = blocks[0].astype(F32)
    for block in blocks[1:]:
        total = total + block.astype(F32)
    return total


def per_device(features, degrees, tile_values, tile_rows, tile_counts, weight, cotangent):
    own_rows, width = features.shape
    col, core = lax.axis_index(COL), lax.axis_index("core")
    columns = jnp.arange(N_COL, dtype=jnp.int32)[:, None, None]
    inv_root = lax.rsqrt(degrees.astype(F32))[:, None]
    scaled = (features.astype(F32) * inv_root).astype(BF)

    one_back = shifted(scaled, 1)
    two_back = shifted(scaled, 2)
    adjacency, flipped = arrange(
        tile_values, tile_rows, tile_counts, jnp.stack([col, core])
    )
    own_or_two = jnp.where(columns >= col, scaled[None], two_back[None])
    offer = jnp.stack([jnp.broadcast_to(one_back[None], own_or_two.shape), own_or_two], axis=1)
    window = lax.all_to_all(offer, COL, 0, 0).reshape(-1, width)

    kept, sent = product(adjacency, window)
    other = lax.ppermute(sent, "core", [(0, 1), (1, 0)])
    half = (kept + other.astype(F32)).astype(BF)
    shares = lax.all_to_all(half.reshape(N_ZH, own_rows, width), "zh", 0, 0)
    own_sum = summed_in_f32(shares)

    aggregated = (own_sum * inv_root).astype(BF)
    pre_act = jnp.dot(aggregated, weight, preferred_element_type=F32)
    sigma = jax.nn.sigmoid(pre_act)
    activations = (pre_act * sigma).astype(BF)
    act_grad = (cotangent.astype(F32) * sigma * (1.0 + pre_act * (1.0 - sigma))).astype(BF)
    back_grad = lax.dot_general(
        act_grad, weight, (((1,), (1,)), ((), ())), preferred_element_type=F32
    )
    back_scaled = (back_grad * inv_root).astype(BF)
    local_weight = lax.dot_general(
        aggregated, act_grad, (((0,), (0,)), ((), ())), preferred_element_type=F32
    ).astype(BF)
    copies = jnp.broadcast_to(back_scaled[None], (N_ZH,) + back_scaled.shape)
    offer = jnp.concatenate([copies, local_weight.reshape(N_ZH, -1, width)], axis=1)
    given = lax.all_to_all(offer, "zh", 0, 0)
    along_zh = given[:, :own_rows].reshape(-1, width)
    weight_part = summed_in_f32(given[:, own_rows:]).astype(BF)
    zh_rows = N_ZH * own_rows
    pair = lax.all_gather(jnp.concatenate([along_zh, weight_part], axis=0), "core")
    slab_grads = pair[:, :zh_rows].reshape(-1, width)
    weight_pair = pair[:, zh_rows:].reshape(N_CORE, N_CORE, -1, width)
    weight_rows = summed_in_f32(lax.dynamic_index_in_dim(weight_pair, core, 1, keepdims=False))

    along_y = copies_to(weight_rows.astype(BF), ROW, N_ROW)
    weight_rows = summed_in_f32(along_y).astype(BF)
    returned = jnp.dot(flipped, slab_grads, preferred_element_type=F32).astype(BF)
    returned = returned.reshape(N_COL, 2 * own_rows, width)
    copies = jnp.broadcast_to(weight_rows[None], (N_COL,) + weight_rows.shape)
    home = lax.all_to_all(jnp.concatenate([returned, copies], axis=1), COL, 0, 0)
    node_total = own_rows * N_ROW * N_COL * N_REP
    weight_rows = (summed_in_f32(home[:, 2 * own_rows :]) / math.sqrt(node_total)).astype(BF)
    along_rep = copies_to(weight_rows, REP, N_REP)
    grad_weight = along_rep.reshape(-1, width).astype(F32)

    arrived = home[:, : 2 * own_rows].reshape(N_COL, 2, own_rows, width)
    for_one = summed_in_f32(arrived[:, 0]).astype(BF)
    nothing = jnp.zeros((), BF)
    for_two = summed_in_f32(jnp.where(columns < col, arrived[:, 1], nothing)).astype(BF)
    for_own = summed_in_f32(jnp.where(columns >= col, arrived[:, 1], nothing))
    from_two = shifted(for_two, -2)
    from_one = shifted(for_one, -1)
    back_total = for_own + from_one.astype(F32) + from_two.astype(F32)
    grad_features = (back_total * inv_root).astype(BF)
    return (activations, grad_weight, grad_features)


def solution(mesh):
    fine = Mesh(
        mesh.devices.reshape(N_ROW, 4, 2, N_ZH, N_CORE), ("y", "x", "zl", "zh", "core")
    )
    nodes = ("y", "x", "zl", "zh", "core")
    placed = (
        P(nodes, None),
        P(nodes),
        P(nodes, None, None, None, None),
        P(nodes, None, None),
        P(nodes, None),
        P(),
        P(nodes, None),
    )

    return jax.shard_map(
        per_device,
        mesh=fine,
        in_specs=placed,
        out_specs=(P(nodes, None), P(), P(nodes, None)),
        check_vma=False,
    )
```

```python
import math

import jax
import jax.numpy as jnp
from jax import lax
from jax.experimental import pallas as pl
from jax.experimental.pallas import tpu as pltpu
from jax.sharding import Mesh, PartitionSpec as P


BF = jnp.bfloat16
F32 = jnp.float32
ROW, COL, REP = "y", ("x", "zl"), ("zh", "core")
N_ROW, N_COL, N_ZH, N_CORE = 8, 8, 4, 2
N_REP = N_ZH * N_CORE


def arrange_kernel(rows_ref, counts_ref, here_ref, tile_hbm, out_ref, flip_ref, tiles, arrived):
    _, span, cap, block, _ = tile_hbm.shape

    def fetch(distance):
        return pltpu.make_async_copy(
            tile_hbm.at[0, distance], tiles.at[distance], arrived.at[distance]
        )

    for distance in range(span):
        fetch(distance).start()
    col, core = here_ref[0], here_ref[1]

    def place_distance(distance, carry):
        fetch(distance).wait()
        live_count = counts_ref[0, distance]
        wrapped = lax.rem(distance, N_COL)
        same_turn = col >= wrapped
        source = jnp.where(same_turn, col - wrapped, col - wrapped + N_COL)
        near = distance < N_COL
        slot = jnp.where(same_turn == near, 1, 0)
        at_col = pl.ds(pl.multiple_of((source * 2 + slot) * block, block), block)
        for k in range(cap):
            owner = rows_ref[0, distance, k]
            owner_core, owner_zh = lax.rem(owner, N_CORE), lax.div(owner, N_CORE)
            far = jnp.where(owner_core == core, 0, N_ZH)
            at_row = pl.ds(pl.multiple_of((far + owner_zh) * block, block), block)
            at_flip = pl.ds(pl.multiple_of((owner_core * N_ZH + owner_zh) * block, block), block)
            tile = tiles[distance, k]
            tile = jnp.where(k < live_count, tile, jnp.zeros_like(tile))
            out_ref[at_row, at_col] = tile
            flip_ref[at_col, at_flip] = tile.T
        return carry

    lax.fori_loop(0, span, place_distance, 0)


def arrange(tile_values, tile_rows, tile_counts, here):
    _, span, cap, rows, cols = tile_values.shape
    size = span * cap * rows * cols
    whole = pl.BlockSpec(memory_space=pltpu.VMEM)
    scalars = pl.BlockSpec(memory_space=pltpu.SMEM)
    return pl.pallas_call(
        arrange_kernel,
        out_shape=(
            jax.ShapeDtypeStruct((cap * rows, span * cols), BF),
            jax.ShapeDtypeStruct((span * cols, cap * rows), BF),
        ),
        in_specs=[scalars, scalars, scalars, pl.BlockSpec(memory_space=pltpu.HBM)],
        out_specs=(whole, whole),
        scratch_shapes=[
            pltpu.VMEM((span, cap, rows, cols), BF),
            pltpu.SemaphoreType.DMA((span,)),
        ],
        cost_estimate=pl.CostEstimate(flops=size, bytes_accessed=4 * size, transcendentals=0),
        name="arrange_tiles",
    )(tile_rows, tile_counts, here, tile_values)


def shifted(block, distance):
    return lax.ppermute(block, ROW, [((i - distance) % N_ROW, i) for i in range(N_ROW)])


def copies_to(block, axis, count):
    return lax.all_to_all(jnp.broadcast_to(block[None], (count,) + block.shape), axis, 0, 0)


def summed_in_f32(blocks):
    total = blocks[0].astype(F32)
    for block in blocks[1:]:
        total = total + block.astype(F32)
    return total


def per_device(features, degrees, tile_values, tile_rows, tile_counts, weight, cotangent):
    own_rows, width = features.shape
    col, core = lax.axis_index(COL), lax.axis_index("core")
    columns = jnp.arange(N_COL, dtype=jnp.int32)[:, None, None]
    inv_root = lax.rsqrt(degrees.astype(F32))[:, None]
    scaled = (features.astype(F32) * inv_root).astype(BF)

    one_back = shifted(scaled, 1)
    two_back = shifted(scaled, 2)
    adjacency, flipped = arrange(
        tile_values, tile_rows, tile_counts, jnp.stack([col, core])
    )
    own_or_two = jnp.where(columns >= col, scaled[None], two_back[None])
    offer = jnp.stack([jnp.broadcast_to(one_back[None], own_or_two.shape), own_or_two], axis=1)
    window = lax.all_to_all(offer, COL, 0, 0).reshape(-1, width)

    partial = jnp.dot(adjacency, window, preferred_element_type=F32)
    kept, sent = jnp.split(partial, 2, axis=0)
    other = lax.ppermute(sent.astype(BF), "core", [(0, 1), (1, 0)])
    half = (kept + other.astype(F32)).astype(BF)
    shares = lax.all_to_all(half.reshape(N_ZH, own_rows, width), "zh", 0, 0)
    own_sum = summed_in_f32(shares)

    aggregated = (own_sum * inv_root).astype(BF)
    pre_act = jnp.dot(aggregated, weight, preferred_element_type=F32)
    sigma = jax.nn.sigmoid(pre_act)
    activations = (pre_act * sigma).astype(BF)
    act_grad = (cotangent.astype(F32) * sigma * (1.0 + pre_act * (1.0 - sigma))).astype(BF)
    back_grad = lax.dot_general(
        act_grad, weight, (((1,), (1,)), ((), ())), preferred_element_type=F32
    )
    back_scaled = (back_grad * inv_root).astype(BF)
    local_weight = lax.dot_general(
        aggregated, act_grad, (((0,), (0,)), ((), ())), preferred_element_type=F32
    ).astype(BF)
    copies = jnp.broadcast_to(back_scaled[None], (N_ZH,) + back_scaled.shape)
    offer = jnp.concatenate([copies, local_weight.reshape(N_ZH, -1, width)], axis=1)
    given = lax.all_to_all(offer, "zh", 0, 0)
    along_zh = given[:, :own_rows].reshape(-1, width)
    weight_part = summed_in_f32(given[:, own_rows:]).astype(BF)
    zh_rows = N_ZH * own_rows
    pair = lax.all_gather(jnp.concatenate([along_zh, weight_part], axis=0), "core")
    slab_grads = pair[:, :zh_rows].reshape(-1, width)
    weight_pair = pair[:, zh_rows:].reshape(N_CORE, N_CORE, -1, width)
    weight_rows = summed_in_f32(lax.dynamic_index_in_dim(weight_pair, core, 1, keepdims=False))

    along_col = copies_to(weight_rows.astype(BF), COL, N_COL)
    weight_rows = summed_in_f32(along_col)
    returned = jnp.dot(flipped, slab_grads, preferred_element_type=F32).astype(BF)
    arrived = lax.all_to_all(returned.reshape(N_COL, 2, own_rows, width), COL, 0, 0)
    along_y = lax.all_gather(weight_rows.astype(BF), ROW)
    node_total = own_rows * N_ROW * N_COL * N_REP
    weight_rows = (summed_in_f32(along_y) / math.sqrt(node_total)).astype(BF)
    along_rep = copies_to(weight_rows, REP, N_REP)
    grad_weight = along_rep.reshape(-1, width).astype(F32)

    for_one = summed_in_f32(arrived[:, 0]).astype(BF)
    nothing = jnp.zeros((), BF)
    for_two = summed_in_f32(jnp.where(columns < col, arrived[:, 1], nothing)).astype(BF)
    for_own = summed_in_f32(jnp.where(columns >= col, arrived[:, 1], nothing))
    from_two = shifted(for_two, -2)
    from_one = shifted(for_one, -1)
    back_total = for_own + from_one.astype(F32) + from_two.astype(F32)
    grad_features = (back_total * inv_root).astype(BF)
    return (activations, grad_weight, grad_features)


def solution(mesh):
    fine = Mesh(
        mesh.devices.reshape(N_ROW, 4, 2, N_ZH, N_CORE), ("y", "x", "zl", "zh", "core")
    )
    nodes = ("y", "x", "zl", "zh", "core")
    placed = (
        P(nodes, None),
        P(nodes),
        P(nodes, None, None, None, None),
        P(nodes, None, None),
        P(nodes, None),
        P(),
        P(nodes, None),
    )

    return jax.shard_map(
        per_device,
        mesh=fine,
        in_specs=placed,
        out_specs=(P(nodes, None), P(), P(nodes, None)),
        check_vma=False,
    )
```

```python
import math

import jax
import jax.numpy as jnp
from jax import lax
from jax.experimental import pallas as pl
from jax.experimental.pallas import tpu as pltpu
from jax.sharding import Mesh, PartitionSpec as P


BF = jnp.bfloat16
F32 = jnp.float32
ROW, COL, REP = ("yp", "ye"), ("x", "zl"), ("zh", "core")
N_PAIR, N_ROW, N_COL, N_ZH, N_CORE = 4, 8, 8, 4, 2
N_REP = N_ZH * N_CORE


def arrange_kernel(rows_ref, counts_ref, here_ref, tile_hbm, out_ref, flip_ref, tiles, arrived):
    _, span, cap, block, _ = tile_hbm.shape

    def fetch(distance):
        return pltpu.make_async_copy(
            tile_hbm.at[0, distance], tiles.at[distance], arrived.at[distance]
        )

    for distance in range(span):
        fetch(distance).start()
    col, core = here_ref[0], here_ref[1]

    def place_distance(distance, carry):
        fetch(distance).wait()
        live_count = counts_ref[0, distance]
        wrapped = lax.rem(distance, N_COL)
        same_turn = col >= wrapped
        source = jnp.where(same_turn, col - wrapped, col - wrapped + N_COL)
        near = distance < N_COL
        slot = jnp.where(same_turn == near, 1, 0)
        at_col = pl.ds(pl.multiple_of((source * 2 + slot) * block, block), block)
        for k in range(cap):
            owner = rows_ref[0, distance, k]
            owner_core, owner_zh = lax.rem(owner, N_CORE), lax.div(owner, N_CORE)
            far = jnp.where(owner_core == core, 0, N_ZH)
            at_row = pl.ds(pl.multiple_of((far + owner_zh) * block, block), block)
            at_flip = pl.ds(pl.multiple_of((owner_core * N_ZH + owner_zh) * block, block), block)
            tile = tiles[distance, k]
            tile = jnp.where(k < live_count, tile, jnp.zeros_like(tile))
            out_ref[at_row, at_col] = tile
            flip_ref[at_col, at_flip] = tile.T
        return carry

    lax.fori_loop(0, span, place_distance, 0)


def arrange(tile_values, tile_rows, tile_counts, here):
    _, span, cap, rows, cols = tile_values.shape
    size = span * cap * rows * cols
    whole = pl.BlockSpec(memory_space=pltpu.VMEM)
    scalars = pl.BlockSpec(memory_space=pltpu.SMEM)
    return pl.pallas_call(
        arrange_kernel,
        out_shape=(
            jax.ShapeDtypeStruct((cap * rows, span * cols), BF),
            jax.ShapeDtypeStruct((span * cols, cap * rows), BF),
        ),
        in_specs=[scalars, scalars, scalars, pl.BlockSpec(memory_space=pltpu.HBM)],
        out_specs=(whole, whole),
        scratch_shapes=[
            pltpu.VMEM((span, cap, rows, cols), BF),
            pltpu.SemaphoreType.DMA((span,)),
        ],
        cost_estimate=pl.CostEstimate(flops=size, bytes_accessed=4 * size, transcendentals=0),
        name="arrange_tiles",
    )(tile_rows, tile_counts, here, tile_values)


def shifted(block, distance):
    return lax.ppermute(block, ROW, [((i - distance) % N_ROW, i) for i in range(N_ROW)])


def copies_to(block, axis, count):
    return lax.all_to_all(jnp.broadcast_to(block[None], (count,) + block.shape), axis, 0, 0)


def summed_in_f32(blocks):
    total = blocks[0].astype(F32)
    for block in blocks[1:]:
        total = total + block.astype(F32)
    return total


def per_device(features, degrees, tile_values, tile_rows, tile_counts, weight, cotangent):
    own_rows, width = features.shape
    col, core = lax.axis_index(COL), lax.axis_index("core")
    columns = jnp.arange(N_COL, dtype=jnp.int32)[:, None, None]
    inv_root = lax.rsqrt(degrees.astype(F32))[:, None]
    scaled = (features.astype(F32) * inv_root).astype(BF)

    one_back = shifted(scaled, 1)
    two_back = shifted(scaled, 2)
    adjacency, flipped = arrange(
        tile_values, tile_rows, tile_counts, jnp.stack([col, core])
    )
    own_or_two = jnp.where(columns >= col, scaled[None], two_back[None])
    offer = jnp.stack([jnp.broadcast_to(one_back[None], own_or_two.shape), own_or_two], axis=1)
    window = lax.all_to_all(offer, COL, 0, 0).reshape(-1, width)

    partial = jnp.dot(adjacency, window, preferred_element_type=F32)
    kept, sent = jnp.split(partial, 2, axis=0)
    other = lax.ppermute(sent.astype(BF), "core", [(0, 1), (1, 0)])
    half = (kept + other.astype(F32)).astype(BF)
    shares = lax.all_to_all(half.reshape(N_ZH, own_rows, width), "zh", 0, 0)
    own_sum = summed_in_f32(shares)

    aggregated = (own_sum * inv_root).astype(BF)
    pre_act = jnp.dot(aggregated, weight, preferred_element_type=F32)
    sigma = jax.nn.sigmoid(pre_act)
    activations = (pre_act * sigma).astype(BF)
    act_grad = (cotangent.astype(F32) * sigma * (1.0 + pre_act * (1.0 - sigma))).astype(BF)
    back_grad = lax.dot_general(
        act_grad, weight, (((1,), (1,)), ((), ())), preferred_element_type=F32
    )
    back_scaled = (back_grad * inv_root).astype(BF)
    local_weight = lax.dot_general(
        aggregated, act_grad, (((0,), (0,)), ((), ())), preferred_element_type=F32
    ).astype(BF)
    copies = jnp.broadcast_to(back_scaled[None], (N_ZH,) + back_scaled.shape)
    offer = jnp.concatenate([copies, local_weight.reshape(N_ZH, -1, width)], axis=1)
    given = lax.all_to_all(offer, "zh", 0, 0)
    along_zh = given[:, :own_rows].reshape(-1, width)
    weight_part = summed_in_f32(given[:, own_rows:]).astype(BF)
    zh_rows = N_ZH * own_rows
    pair = lax.all_gather(jnp.concatenate([along_zh, weight_part], axis=0), "core")
    slab_grads = pair[:, :zh_rows].reshape(-1, width)
    weight_pair = pair[:, zh_rows:].reshape(N_CORE, N_CORE, -1, width)
    weight_rows = summed_in_f32(lax.dynamic_index_in_dim(weight_pair, core, 1, keepdims=False))

    along_col = copies_to(weight_rows.astype(BF), ("ye",) + COL, N_ROW // N_PAIR * N_COL)
    weight_rows = summed_in_f32(along_col)
    returned = jnp.dot(flipped, slab_grads, preferred_element_type=F32).astype(BF)
    arrived = lax.all_to_all(returned.reshape(N_COL, 2, own_rows, width), COL, 0, 0)
    own_part = weight_rows.astype(BF)
    parts = [own_part]
    for away in range(1, N_PAIR):
        route = [((i - away) % N_PAIR, i) for i in range(N_PAIR)]
        parts.append(lax.ppermute(own_part, "yp", route))
    node_total = own_rows * N_ROW * N_COL * N_REP
    weight_rows = (summed_in_f32(parts) / math.sqrt(node_total)).astype(BF)
    along_rep = copies_to(weight_rows, REP, N_REP)
    grad_weight = along_rep.reshape(-1, width).astype(F32)

    for_one = summed_in_f32(arrived[:, 0]).astype(BF)
    nothing = jnp.zeros((), BF)
    for_two = summed_in_f32(jnp.where(columns < col, arrived[:, 1], nothing)).astype(BF)
    for_own = summed_in_f32(jnp.where(columns >= col, arrived[:, 1], nothing))
    from_two = shifted(for_two, -2)
    from_one = shifted(for_one, -1)
    back_total = for_own + from_one.astype(F32) + from_two.astype(F32)
    grad_features = (back_total * inv_root).astype(BF)
    return (activations, grad_weight, grad_features)


def solution(mesh):
    fine = Mesh(
        mesh.devices.reshape(N_PAIR, 2, 4, 2, N_ZH, N_CORE), ROW + COL + REP
    )
    nodes = ROW + COL + REP
    placed = (
        P(nodes, None),
        P(nodes),
        P(nodes, None, None, None, None),
        P(nodes, None, None),
        P(nodes, None),
        P(),
        P(nodes, None),
    )

    return jax.shard_map(
        per_device,
        mesh=fine,
        in_specs=placed,
        out_specs=(P(nodes, None), P(), P(nodes, None)),
        check_vma=False,
    )
```

```python
import math

import jax
import jax.numpy as jnp
from jax import lax
from jax.experimental import pallas as pl
from jax.experimental.pallas import tpu as pltpu
from jax.sharding import Mesh, PartitionSpec as P


BF = jnp.bfloat16
F32 = jnp.float32
PAIR, GROUP, REP = "yp", ("ye", "x", "zl"), ("zh", "core")
N_PAIR, N_GROUP, N_ZH, N_CORE = 4, 16, 4, 2
N_REP = N_ZH * N_CORE


def arrange_kernel(rows_ref, counts_ref, here_ref, tile_hbm, out_ref, flip_ref, tiles, arrived):
    _, span, cap, block, _ = tile_hbm.shape

    def fetch(distance):
        return pltpu.make_async_copy(
            tile_hbm.at[0, distance], tiles.at[distance], arrived.at[distance]
        )

    for distance in range(span):
        fetch(distance).start()
    place, core = here_ref[0], here_ref[1]

    def place_distance(distance, carry):
        fetch(distance).wait()
        live_count = counts_ref[0, distance]
        source = lax.rem(place + (span - distance), span)
        at_col = pl.ds(pl.multiple_of(source * block, block), block)
        for k in range(cap):
            owner = rows_ref[0, distance, k]
            owner_core, owner_zh = lax.rem(owner, N_CORE), lax.div(owner, N_CORE)
            far = jnp.where(owner_core == core, 0, N_ZH)
            at_row = pl.ds(pl.multiple_of((far + owner_zh) * block, block), block)
            at_flip = pl.ds(pl.multiple_of((owner_core * N_ZH + owner_zh) * block, block), block)
            tile = tiles[distance, k]
            tile = jnp.where(k < live_count, tile, jnp.zeros_like(tile))
            out_ref[at_row, at_col] = tile
            flip_ref[at_col, at_flip] = tile.T
        return carry

    lax.fori_loop(0, span, place_distance, 0)


def arrange(tile_values, tile_rows, tile_counts, here):
    _, span, cap, rows, cols = tile_values.shape
    size = span * cap * rows * cols
    whole = pl.BlockSpec(memory_space=pltpu.VMEM)
    scalars = pl.BlockSpec(memory_space=pltpu.SMEM)
    return pl.pallas_call(
        arrange_kernel,
        out_shape=(
            jax.ShapeDtypeStruct((cap * rows, span * cols), BF),
            jax.ShapeDtypeStruct((span * cols, cap * rows), BF),
        ),
        in_specs=[scalars, scalars, scalars, pl.BlockSpec(memory_space=pltpu.HBM)],
        out_specs=(whole, whole),
        scratch_shapes=[
            pltpu.VMEM((span, cap, rows, cols), BF),
            pltpu.SemaphoreType.DMA((span,)),
        ],
        cost_estimate=pl.CostEstimate(flops=size, bytes_accessed=4 * size, transcendentals=0),
        name="arrange_tiles",
    )(tile_rows, tile_counts, here, tile_values)


def shifted(block, distance):
    return lax.ppermute(block, PAIR, [((i - distance) % N_PAIR, i) for i in range(N_PAIR)])


def copies_to(block, axis, count):
    return lax.all_to_all(jnp.broadcast_to(block[None], (count,) + block.shape), axis, 0, 0)


def summed_in_f32(blocks):
    total = blocks[0].astype(F32)
    for block in blocks[1:]:
        total = total + block.astype(F32)
    return total


def per_device(features, degrees, tile_values, tile_rows, tile_counts, weight, cotangent):
    own_rows, width = features.shape
    place, core = lax.axis_index(GROUP), lax.axis_index("core")
    places = jnp.arange(N_GROUP, dtype=jnp.int32)[:, None, None]
    inv_root = lax.rsqrt(degrees.astype(F32))[:, None]
    scaled = (features.astype(F32) * inv_root).astype(BF)

    pair_back = shifted(scaled, 1)
    adjacency, flipped = arrange(
        tile_values, tile_rows, tile_counts, jnp.stack([place, core])
    )
    offer = jnp.where(places >= place, scaled[None], pair_back[None])
    window = lax.all_to_all(offer, GROUP, 0, 0).reshape(-1, width)

    partial = jnp.dot(adjacency, window, preferred_element_type=F32)
    kept, sent = jnp.split(partial, 2, axis=0)
    other = lax.ppermute(sent.astype(BF), "core", [(0, 1), (1, 0)])
    half = (kept + other.astype(F32)).astype(BF)
    shares = lax.all_to_all(half.reshape(N_ZH, own_rows, width), "zh", 0, 0)
    own_sum = summed_in_f32(shares)

    aggregated = (own_sum * inv_root).astype(BF)
    pre_act = jnp.dot(aggregated, weight, preferred_element_type=F32)
    sigma = jax.nn.sigmoid(pre_act)
    activations = (pre_act * sigma).astype(BF)
    act_grad = (cotangent.astype(F32) * sigma * (1.0 + pre_act * (1.0 - sigma))).astype(BF)
    back_grad = lax.dot_general(
        act_grad, weight, (((1,), (1,)), ((), ())), preferred_element_type=F32
    )
    back_scaled = (back_grad * inv_root).astype(BF)
    local_weight = lax.dot_general(
        aggregated, act_grad, (((0,), (0,)), ((), ())), preferred_element_type=F32
    ).astype(BF)
    copies = jnp.broadcast_to(back_scaled[None], (N_ZH,) + back_scaled.shape)
    offer = jnp.concatenate([copies, local_weight.reshape(N_ZH, -1, width)], axis=1)
    given = lax.all_to_all(offer, "zh", 0, 0)
    along_zh = given[:, :own_rows].reshape(-1, width)
    weight_part = summed_in_f32(given[:, own_rows:]).astype(BF)
    zh_rows = N_ZH * own_rows
    pair = lax.all_gather(jnp.concatenate([along_zh, weight_part], axis=0), "core")
    slab_grads = pair[:, :zh_rows].reshape(-1, width)
    weight_pair = pair[:, zh_rows:].reshape(N_CORE, N_CORE, -1, width)
    weight_rows = summed_in_f32(lax.dynamic_index_in_dim(weight_pair, core, 1, keepdims=False))

    along_group = copies_to(weight_rows.astype(BF), GROUP, N_GROUP)
    weight_rows = summed_in_f32(along_group)
    returned = jnp.dot(flipped, slab_grads, preferred_element_type=F32).astype(BF)
    arrived = lax.all_to_all(returned.reshape(N_GROUP, own_rows, width), GROUP, 0, 0)
    own_part = weight_rows.astype(BF)
    parts = [own_part] + [shifted(own_part, away) for away in range(1, N_PAIR)]
    node_total = own_rows * N_PAIR * N_GROUP * N_REP
    weight_rows = (summed_in_f32(parts) / math.sqrt(node_total)).astype(BF)
    along_rep = copies_to(weight_rows, REP, N_REP)
    grad_weight = along_rep.reshape(-1, width).astype(F32)

    nothing = jnp.zeros((), BF)
    for_back = summed_in_f32(jnp.where(places < place, arrived, nothing)).astype(BF)
    for_own = summed_in_f32(jnp.where(places >= place, arrived, nothing))
    from_next = shifted(for_back, -1)
    back_total = for_own + from_next.astype(F32)
    grad_features = (back_total * inv_root).astype(BF)
    return (activations, grad_weight, grad_features)


def solution(mesh):
    fine = Mesh(
        mesh.devices.reshape(N_PAIR, 2, 4, 2, N_ZH, N_CORE), (PAIR,) + GROUP + REP
    )
    nodes = (PAIR,) + GROUP + REP
    placed = (
        P(nodes, None),
        P(nodes),
        P(nodes, None, None, None, None),
        P(nodes, None, None),
        P(nodes, None),
        P(),
        P(nodes, None),
    )

    return jax.shard_map(
        per_device,
        mesh=fine,
        in_specs=placed,
        out_specs=(P(nodes, None), P(), P(nodes, None)),
        check_vma=False,
    )
```

```python
import math

import jax
import jax.numpy as jnp
from jax import lax
from jax.experimental import pallas as pl
from jax.experimental.pallas import tpu as pltpu
from jax.sharding import Mesh, PartitionSpec as P


BF = jnp.bfloat16
F32 = jnp.float32
PAIR, GROUP, REP = "yp", ("ye", "x", "zl"), ("zh", "core")
N_PAIR, N_GROUP, N_ZH, N_CORE = 4, 16, 4, 2
N_REP = N_ZH * N_CORE


def arrange_kernel(rows_ref, counts_ref, here_ref, tile_hbm, out_ref, flip_ref, tiles, arrived):
    _, span, cap, block, _ = tile_hbm.shape

    def fetch(distance):
        return pltpu.make_async_copy(
            tile_hbm.at[0, distance], tiles.at[distance], arrived.at[distance]
        )

    for distance in range(span):
        fetch(distance).start()
    place, core = here_ref[0], here_ref[1]

    def place_distance(distance, carry):
        fetch(distance).wait()
        live_count = counts_ref[0, distance]
        source = lax.rem(place + (span - distance), span)
        at_col = pl.ds(pl.multiple_of(source * block, block), block)
        for k in range(cap):
            owner = rows_ref[0, distance, k]
            owner_core, owner_zh = lax.rem(owner, N_CORE), lax.div(owner, N_CORE)
            far = jnp.where(owner_core == core, 0, N_ZH)
            at_row = pl.ds(pl.multiple_of((far + owner_zh) * block, block), block)
            at_flip = pl.ds(pl.multiple_of((owner_core * N_ZH + owner_zh) * block, block), block)
            tile = tiles[distance, k]
            tile = jnp.where(k < live_count, tile, jnp.zeros_like(tile))
            out_ref[at_row, at_col] = tile
            flip_ref[at_col, at_flip] = tile.T
        return carry

    lax.fori_loop(0, span, place_distance, 0)


def arrange(tile_values, tile_rows, tile_counts, here):
    _, span, cap, rows, cols = tile_values.shape
    size = span * cap * rows * cols
    whole = pl.BlockSpec(memory_space=pltpu.VMEM)
    scalars = pl.BlockSpec(memory_space=pltpu.SMEM)
    return pl.pallas_call(
        arrange_kernel,
        out_shape=(
            jax.ShapeDtypeStruct((cap * rows, span * cols), BF),
            jax.ShapeDtypeStruct((span * cols, cap * rows), BF),
        ),
        in_specs=[scalars, scalars, scalars, pl.BlockSpec(memory_space=pltpu.HBM)],
        out_specs=(whole, whole),
        scratch_shapes=[
            pltpu.VMEM((span, cap, rows, cols), BF),
            pltpu.SemaphoreType.DMA((span,)),
        ],
        cost_estimate=pl.CostEstimate(flops=size, bytes_accessed=4 * size, transcendentals=0),
        name="arrange_tiles",
    )(tile_rows, tile_counts, here, tile_values)


def scale_kernel(degrees_ref, features_ref, scaled_ref, root_ref):
    rows, width = features_ref.shape
    root = lax.rsqrt(degrees_ref[...].astype(F32))
    root_ref[...] = root
    across = jnp.broadcast_to(root, (rows, rows)).T
    for start in range(0, width, rows):
        lanes = pl.ds(start, rows)
        scaled_ref[:, lanes] = (features_ref[:, lanes].astype(F32) * across).astype(BF)


def scaled_rows(features, degrees):
    rows, width = features.shape
    return pl.pallas_call(
        scale_kernel,
        out_shape=(pltpu.VMEM((rows, width), BF), pltpu.VMEM((1, rows), F32)),
        in_specs=[pl.BlockSpec(memory_space=pltpu.VMEM)] * 2,
        out_specs=(pl.BlockSpec(memory_space=pltpu.VMEM),) * 2,
        cost_estimate=pl.CostEstimate(
            flops=rows * width, bytes_accessed=4 * rows * width, transcendentals=rows
        ),
        name="scale_rows",
    )(degrees[None, :], features)


def dense_kernel(shares_ref, root_ref, weight_ref, cotangent_ref, act_ref, offer_ref):
    rows, width = act_ref.shape
    across = jnp.broadcast_to(root_ref[...], (rows, rows)).T
    across = jnp.concatenate([across] * (width // rows), axis=1)
    aggregated = (summed_in_f32(shares_ref) * across).astype(BF)
    pre_act = jnp.dot(aggregated, weight_ref[...], preferred_element_type=F32)
    sigma = jax.nn.sigmoid(pre_act)
    act_ref[...] = (pre_act * sigma).astype(BF)
    cotangent = cotangent_ref[...].astype(F32)
    act_grad = (cotangent * sigma * (1.0 + pre_act * (1.0 - sigma))).astype(BF)
    back_grad = lax.dot_general(
        act_grad, weight_ref[...], (((1,), (1,)), ((), ())), preferred_element_type=F32
    )
    back_scaled = (back_grad * across).astype(BF)
    local_weight = lax.dot_general(
        aggregated, act_grad, (((0,), (0,)), ((), ())), preferred_element_type=F32
    ).astype(BF)
    share = width // N_ZH
    for zh in range(N_ZH):
        offer_ref[zh, :rows] = back_scaled
        offer_ref[zh, rows:] = local_weight[zh * share : (zh + 1) * share]


def dense(shares, root, weight, cotangent):
    rows, width = cotangent.shape
    whole = pl.BlockSpec(memory_space=pltpu.VMEM)
    return pl.pallas_call(
        dense_kernel,
        out_shape=(
            jax.ShapeDtypeStruct((rows, width), BF),
            pltpu.VMEM((N_ZH, rows + width // N_ZH, width), BF),
        ),
        in_specs=[whole] * 4,
        out_specs=(whole, whole),
        cost_estimate=pl.CostEstimate(
            flops=6 * rows * width * width,
            bytes_accessed=16 * rows * width,
            transcendentals=rows * width,
        ),
        compiler_params=pltpu.CompilerParams(vmem_limit_bytes=8 * 2**20),
        name="dense_part",
    )(shares, root, weight, cotangent)


def shifted(block, distance):
    return lax.ppermute(block, PAIR, [((i - distance) % N_PAIR, i) for i in range(N_PAIR)])


def copies_to(block, axis, count):
    return lax.all_to_all(jnp.broadcast_to(block[None], (count,) + block.shape), axis, 0, 0)


def summed_in_f32(blocks):
    total = blocks[0].astype(F32)
    for index in range(1, len(blocks) if isinstance(blocks, list) else blocks.shape[0]):
        total = total + blocks[index].astype(F32)
    return total


def per_device(features, degrees, tile_values, tile_rows, tile_counts, weight, cotangent):
    own_rows, width = features.shape
    place, core = lax.axis_index(GROUP), lax.axis_index("core")
    places = jnp.arange(N_GROUP, dtype=jnp.int32)[:, None, None]
    scaled, root = scaled_rows(features, degrees)
    inv_root = root[0][:, None]

    pair_back = shifted(scaled, 1)
    adjacency, flipped = arrange(
        tile_values, tile_rows, tile_counts, jnp.stack([place, core])
    )
    offer = jnp.where(places >= place, scaled[None], pair_back[None])
    window = lax.all_to_all(offer, GROUP, 0, 0).reshape(-1, width)

    partial = jnp.dot(adjacency, window, preferred_element_type=F32)
    kept, sent = jnp.split(partial, 2, axis=0)
    other = lax.ppermute(sent.astype(BF), "core", [(0, 1), (1, 0)])
    half = (kept + other.astype(F32)).astype(BF)
    shares = lax.all_to_all(half.reshape(N_ZH, own_rows, width), "zh", 0, 0)
    activations, offer = dense(shares, root, weight, cotangent)
    given = lax.all_to_all(offer, "zh", 0, 0)
    along_zh = given[:, :own_rows].reshape(-1, width)
    weight_part = summed_in_f32(given[:, own_rows:]).astype(BF)
    zh_rows = N_ZH * own_rows
    pair = lax.all_gather(jnp.concatenate([along_zh, weight_part], axis=0), "core")
    slab_grads = pair[:, :zh_rows].reshape(-1, width)
    weight_pair = pair[:, zh_rows:].reshape(N_CORE, N_CORE, -1, width)
    weight_rows = summed_in_f32(lax.dynamic_index_in_dim(weight_pair, core, 1, keepdims=False))

    along_group = copies_to(weight_rows.astype(BF), GROUP, N_GROUP)
    weight_rows = summed_in_f32(along_group)
    returned = jnp.dot(flipped, slab_grads, preferred_element_type=F32).astype(BF)
    arrived = lax.all_to_all(returned.reshape(N_GROUP, own_rows, width), GROUP, 0, 0)
    own_part = weight_rows.astype(BF)
    parts = [own_part] + [shifted(own_part, away) for away in range(1, N_PAIR)]
    node_total = own_rows * N_PAIR * N_GROUP * N_REP
    weight_rows = (summed_in_f32(parts) / math.sqrt(node_total)).astype(BF)
    along_rep = copies_to(weight_rows, REP, N_REP)
    grad_weight = along_rep.reshape(-1, width).astype(F32)

    nothing = jnp.zeros((), BF)
    for_back = summed_in_f32(jnp.where(places < place, arrived, nothing)).astype(BF)
    for_own = summed_in_f32(jnp.where(places >= place, arrived, nothing))
    from_next = shifted(for_back, -1)
    back_total = for_own + from_next.astype(F32)
    grad_features = (back_total * inv_root).astype(BF)
    return (activations, grad_weight, grad_features)


def solution(mesh):
    fine = Mesh(
        mesh.devices.reshape(N_PAIR, 2, 4, 2, N_ZH, N_CORE), (PAIR,) + GROUP + REP
    )
    nodes = (PAIR,) + GROUP + REP
    placed = (
        P(nodes, None),
        P(nodes),
        P(nodes, None, None, None, None),
        P(nodes, None, None),
        P(nodes, None),
        P(),
        P(nodes, None),
    )

    return jax.shard_map(
        per_device,
        mesh=fine,
        in_specs=placed,
        out_specs=(P(nodes, None), P(), P(nodes, None)),
        check_vma=False,
    )
```
